768 devices in a mesh: dp: 32 (over y, x), tensor: 24 (over z, core).
Axes of the slice: x: 4, y: 8, z: 12, core: 2. Of those that a mesh axis runs over, the one named last changes fastest.
Arguments:
- kept_input: bfloat16 [18432, 4096], P(('dp', 'tensor')), may hold values from -6 to 6
- kept_grad: bfloat16 [18432, 4096], P(('dp', 'tensor')), may hold values from -6 to 6
- up_weight_t: bfloat16 [8256, 4096], P('tensor'), may hold values from -0.09375 to 0.09375
- up_bias: bfloat16 [8256], P('tensor'), may hold values from -4 to 4
- down_weight: bfloat16 [8256, 4096], P('tensor'), may hold values from -0.0625 to 0.0625
- kept_count: int32 [768], P(('dp', 'tensor')), may hold values from 8 to 24, as said below
Outputs:
- grad_kept: bfloat16 [18432, 4096], P(('dp', 'tensor'))
The draws below stay inside these ranges and needn't reach their ends.
Inputs may be any that keep to these rules, and one draw needn't show every extreme that they name: `kept_count`: every block keeps at least 8 and at most 24 of its 24 slots, some block exactly 24. Among the 32 blocks of one tensor index taken in order of g, the blocks before block g keep g * 16 + e tokens together with e between -4 and 4, and e is 0 for g = 0 and for g = 32 (all 32 blocks together keep exactly 512 tokens).
All inputs are finite; a program needn't handle non-finite values.
Results may differ from the reference program's by a relative error of at most 0.014.
Values may be sent and summed in bfloat16 or wider, within the bound.
No kernel may reach another device: no remote copies, remote signals or barrier semaphores. Data moves between devices by JAX's collectives and lax.ppermute only.
A program may use at most 64 MiB of HBM per device.

```python
import jax
import jax.numpy as jnp
from jax import lax

D = 4096
FF = 8256
BAL = 16
KEPT_ROWS = 18432
N_DP = 32
N_TENSOR = 24


def draw_kept_count(key, part):
    halo_width = BAL // 4
    key_excess, key_pick = jax.random.split(key, 2)
    inner = jax.random.randint(key_excess, (N_DP - 1, N_TENSOR), -halo_width, halo_width + 1)
    chosen = jax.random.randint(key_pick, (1, N_TENSOR), 1, N_DP - 1)
    positions = jnp.arange(1, N_DP, dtype=jnp.int32)[:, None]
    inner = jnp.where(positions == chosen, -halo_width, inner)
    inner = jnp.where(positions == chosen + 1, halo_width, inner)
    border = jnp.zeros((1, N_TENSOR), jnp.int32)
    excess = jnp.concatenate((border, inner.astype(jnp.int32), border), axis=0)
    counts = BAL + excess[1:] - excess[:-1]
    return counts.reshape(-1).astype(jnp.int32)


def steps_of(rng, shape, shards, least, high):
    loudness = 1.0
    for position, shards_of in shards:
        steps = jax.random.uniform(jax.random.fold_in(jax.random.fold_in(rng, 6), position), (shards_of,), jnp.float32, least / len(shards), high / len(shards))
        loudness = loudness * jnp.repeat(jnp.exp(steps), shape[position] // shards_of).reshape((-1,) + (1,) * (len(shape) - 1 - position))
    return loudness


def noise(rng, shape, scale, bound, shards=(), held_as=jnp.bfloat16):
    loudness = steps_of(rng, shape, shards, -0.22, 0.18) if shards else 1.0
    array = jax.random.normal(rng, shape, jnp.float32) * scale * loudness
    return jnp.minimum(jnp.maximum(array, -bound), bound).astype(held_as)


def setup_inputs(seed: int = 0) -> dict:
    key_list = jax.random.split(jax.random.key(seed), 7)
    kept_input = noise(key_list[0], (KEPT_ROWS, D), 1.0, 6.0, ((0, 768),))
    kept_grad = noise(key_list[1], (KEPT_ROWS, D), 1.0, 6.0, ((0, 768),))
    up_weight_t = noise(key_list[2], (FF, D), D ** -0.5, 0.09375, ((0, 24),))
    up_bias = noise(key_list[3], (FF,), 1.0, 4.0, ((0, 24),))
    down_weight = noise(key_list[4], (FF, D), FF ** -0.5, 0.0625, ((0, 24),))
    kept_count = draw_kept_count(jax.random.fold_in(key_list[6], 71), 0)
    return dict(kept_input=kept_input, kept_grad=kept_grad, up_weight_t=up_weight_t, up_bias=up_bias, down_weight=down_weight, kept_count=kept_count)


INV_SQRT_TWO = 0.7071067811865476
INV_SQRT_TWO_PI = 0.3989422804014327


def gelu_slope(values):
    return 0.5 * (1.0 + lax.erf(values * INV_SQRT_TWO)) + values * jnp.exp(-0.5 * values * values) * INV_SQRT_TWO_PI


def reference(kept_input, kept_grad, up_weight_t, up_bias, down_weight, kept_count):
    blocks = kept_count.shape[0]
    slots = kept_input.shape[0] // blocks
    live = jnp.arange(slots, dtype=jnp.int32)[None, :] < kept_count[:, None]
    kept_total = N_DP * N_TENSOR * BAL
    row_ids = jnp.nonzero(live.reshape(-1), size=kept_total)[0].astype(jnp.int32)
    inputs = kept_input[row_ids]
    out_grads = kept_grad[row_ids]
    block_width = FF // N_TENSOR

    def block_term(summed, tensor_rank):
        first_row = tensor_rank * block_width
        up_block = lax.dynamic_slice_in_dim(up_weight_t, first_row, block_width, 0)
        bias_block = lax.dynamic_slice_in_dim(up_bias, first_row, block_width, 0)
        down_block = lax.dynamic_slice_in_dim(down_weight, first_row, block_width, 0)
        preact = jnp.dot(inputs, up_block.T, preferred_element_type=jnp.float32) + bias_block.astype(jnp.float32)
        down_grad = jnp.dot(out_grads, down_block.T, preferred_element_type=jnp.float32)
        pre_grad = (gelu_slope(preact) * down_grad).astype(jnp.bfloat16)
        rounded = jnp.dot(pre_grad, up_block, preferred_element_type=jnp.float32).astype(jnp.bfloat16)
        rounded = lax.optimization_barrier(rounded)
        return summed + rounded.astype(jnp.float32), None

    summed, _ = lax.scan(block_term, jnp.zeros((kept_total, D), jnp.float32), jnp.arange(N_TENSOR, dtype=jnp.int32))
    branch = summed.astype(jnp.bfloat16)
    spread = jnp.zeros(kept_input.shape, jnp.float32).at[row_ids].add(branch.astype(jnp.float32))
    result = jnp.where(live.reshape(-1)[:, None], kept_grad.astype(jnp.float32) + spread, jnp.float32(0.0))
    return result.astype(jnp.bfloat16)
```

```python
import jax
import jax.numpy as jnp
from jax import lax
from jax.sharding import PartitionSpec as P

CORES = 2

INV_SQRT_TWO = 0.7071067811865476
INV_SQRT_TWO_PI = 0.3989422804014327


def gelu_slope(values):
    return (
        0.5 * (1.0 + lax.erf(values * INV_SQRT_TWO))
        + values * jnp.exp(-0.5 * values * values) * INV_SQRT_TWO_PI
    )


def with_sibling(block, pairs):
    return jnp.concatenate([block, lax.ppermute(block, "tensor", pairs)], axis=0)


def body(kept_input, kept_grad, up_weight_t, up_bias, down_weight, kept_count):
    slots = kept_input.shape[0]
    members = lax.axis_size("tensor")
    pairs = [(i, i ^ 1) for i in range(members)]
    rings = [list(range(core, members, CORES)) for core in range(CORES)]
    contract = (((1,), (1,)), ((), ()))

    stacked = jnp.stack((kept_input, kept_grad), axis=1)
    stacked, up_weight_t, up_bias, down_weight = lax.optimization_barrier(
        (stacked, up_weight_t, up_bias, down_weight)
    )
    gathered = lax.all_gather(stacked, "tensor", axis=0, tiled=True, axis_index_groups=rings)

    up = with_sibling(up_weight_t, pairs)
    down = with_sibling(down_weight, pairs)
    bias = with_sibling(up_bias, pairs).astype(jnp.float32)

    inputs = gathered[:, 0]
    out_grads = gathered[:, 1]
    preact = lax.dot_general(inputs, up, contract, preferred_element_type=jnp.float32) + bias
    down_grad = lax.dot_general(out_grads, down, contract, preferred_element_type=jnp.float32)
    pre_grad = (gelu_slope(preact) * down_grad).astype(jnp.bfloat16)
    partials = jnp.dot(pre_grad, up, preferred_element_type=jnp.float32)
    branch = lax.psum_scatter(
        partials.astype(jnp.bfloat16),
        "tensor",
        scatter_dimension=0,
        axis_index_groups=rings,
        tiled=True,
    )
    usable = jnp.arange(slots, dtype=jnp.int32) < kept_count[0]
    summed = kept_grad.astype(jnp.float32) + branch.astype(jnp.float32)
    return jnp.where(usable[:, None], summed, jnp.float32(0.0)).astype(jnp.bfloat16)


def solution(mesh):
    placed = (
        P(("dp", "tensor"), None),
        P(("dp", "tensor"), None),
        P("tensor", None),
        P("tensor"),
        P("tensor", None),
        P(("dp", "tensor")),
    )
    return jax.shard_map(
        body, mesh=mesh, in_specs=placed, out_specs=P(("dp", "tensor"), None), check_vma=False
    )
```

```python
import jax
import jax.numpy as jnp
from jax import lax
from jax.sharding import PartitionSpec as P

CORES = 2

INV_SQRT_TWO = 0.7071067811865476
INV_SQRT_TWO_PI = 0.3989422804014327


def gelu_slope(values):
    return (
        0.5 * (1.0 + lax.erf(values * INV_SQRT_TWO))
        + values * jnp.exp(-0.5 * values * values) * INV_SQRT_TWO_PI
    )


def with_sibling(block, pairs):
    return jnp.concatenate([block, lax.ppermute(block, "tensor", pairs)], axis=0)


def body(kept_input, kept_grad, up_weight_t, up_bias, down_weight, kept_count):
    slots = kept_input.shape[0]
    members = lax.axis_size("tensor")
    pairs = [(i, i ^ 1) for i in range(members)]
    rings = [list(range(core, members, CORES)) for core in range(CORES)]
    chips = members // CORES
    one_side = [(i, i ^ CORES) for i in range(members)]
    other_side = [
        (i, (i - CORES if i // CORES % 2 == 0 else i + CORES) % members) for i in range(members)
    ]
    alike = [list(range(first, members, 2 * CORES)) for first in range(2 * CORES)]
    parity = lax.axis_index("tensor") // CORES % 2
    contract = (((1,), (1,)), ((), ()))

    stacked = jnp.stack((kept_input, kept_grad), axis=1)
    stacked, up_weight_t, up_bias, down_weight = lax.optimization_barrier(
        (stacked, up_weight_t, up_bias, down_weight)
    )
    gathered = lax.all_gather(stacked, "tensor", axis=0, tiled=True, axis_index_groups=rings)

    up = with_sibling(up_weight_t, pairs)
    down = with_sibling(down_weight, pairs)
    bias = with_sibling(up_bias, pairs).astype(jnp.float32)

    inputs = gathered[:, 0]
    out_grads = gathered[:, 1]
    preact = lax.dot_general(inputs, up, contract, preferred_element_type=jnp.float32) + bias
    down_grad = lax.dot_general(out_grads, down, contract, preferred_element_type=jnp.float32)
    pre_grad = (gelu_slope(preact) * down_grad).astype(jnp.bfloat16)
    hidden = pre_grad.shape[1]
    by_parity = pre_grad.reshape(chips // 2, 2, slots, hidden)

    def terms(which):
        chosen = lax.dynamic_index_in_dim(by_parity, which, axis=1, keepdims=False)
        chosen = chosen.reshape(chips // 2 * slots, hidden)
        return jnp.dot(chosen, up, preferred_element_type=jnp.float32).astype(jnp.bfloat16)

    leaving = terms(1 - parity)
    half = leaving.shape[1] // 2
    arrived = jnp.concatenate(
        [
            lax.ppermute(leaving[:, :half], "tensor", one_side),
            lax.ppermute(leaving[:, half:], "tensor", other_side),
        ],
        axis=1,
    )
    staying = lax.optimization_barrier(terms(parity))
    pair_sums = (staying.astype(jnp.float32) + arrived.astype(jnp.float32)).astype(jnp.bfloat16)
    branch = lax.psum_scatter(
        pair_sums, "tensor", scatter_dimension=0, axis_index_groups=alike, tiled=True
    )
    usable = jnp.arange(slots, dtype=jnp.int32) < kept_count[0]
    summed = kept_grad.astype(jnp.float32) + branch.astype(jnp.float32)
    return jnp.where(usable[:, None], summed, jnp.float32(0.0)).astype(jnp.bfloat16)


def solution(mesh):
    placed = (
        P(("dp", "tensor"), None),
        P(("dp", "tensor"), None),
        P("tensor", None),
        P("tensor"),
        P("tensor", None),
        P(("dp", "tensor")),
    )
    return jax.shard_map(
        body, mesh=mesh, in_specs=placed, out_specs=P(("dp", "tensor"), None), check_vma=False
    )
```

```python
import jax
import jax.numpy as jnp
from jax import lax
from jax.sharding import PartitionSpec as P

CORES = 2

INV_SQRT_TWO = 0.7071067811865476
INV_SQRT_TWO_PI = 0.3989422804014327


def gelu_slope(values):
    return (
        0.5 * (1.0 + lax.erf(values * INV_SQRT_TWO))
        + values * jnp.exp(-0.5 * values * values) * INV_SQRT_TWO_PI
    )


def with_sibling(block, pairs):
    return jnp.concatenate([block, lax.ppermute(block, "tensor", pairs)], axis=0)


def body(kept_input, kept_grad, up_weight_t, up_bias, down_weight, kept_count):
    slots = kept_input.shape[0]
    members = lax.axis_size("tensor")
    pairs = [(i, i ^ 1) for i in range(members)]
    rings = [list(range(core, members, CORES)) for core in range(CORES)]
    contract = (((1,), (1,)), ((), ()))

    stacked = jnp.stack((kept_input, kept_grad), axis=1)
    stacked, up_weight_t, up_bias, down_weight = lax.optimization_barrier(
        (stacked, up_weight_t, up_bias, down_weight)
    )
    gathered = lax.all_gather(stacked, "tensor", axis=0, tiled=True, axis_index_groups=rings)

    up = with_sibling(up_weight_t, pairs)
    down = with_sibling(down_weight, pairs)
    bias = with_sibling(up_bias, pairs).astype(jnp.float32)

    inputs = gathered[:, 0]
    out_grads = gathered[:, 1]
    preact = lax.dot_general(inputs, up, contract, preferred_element_type=jnp.float32) + bias
    down_grad = lax.dot_general(out_grads, down, contract, preferred_element_type=jnp.float32)
    pre_grad = lax.optimization_barrier((gelu_slope(preact) * down_grad).astype(jnp.bfloat16))
    partials = jnp.dot(pre_grad, up, preferred_element_type=jnp.float32)
    branch = lax.psum_scatter(
        partials.astype(jnp.bfloat16),
        "tensor",
        scatter_dimension=0,
        axis_index_groups=rings,
        tiled=True,
    )
    usable = jnp.arange(slots, dtype=jnp.int32) < kept_count[0]
    summed = kept_grad.astype(jnp.float32) + branch.astype(jnp.float32)
    return jnp.where(usable[:, None], summed, jnp.float32(0.0)).astype(jnp.bfloat16)


def solution(mesh):
    placed = (
        P(("dp", "tensor"), None),
        P(("dp", "tensor"), None),
        P("tensor", None),
        P("tensor"),
        P("tensor", None),
        P(("dp", "tensor")),
    )
    return jax.shard_map(
        body, mesh=mesh, in_specs=placed, out_specs=P(("dp", "tensor"), None), check_vma=False
    )
```

```python
import jax
import jax.numpy as jnp
from jax import lax
from jax.sharding import PartitionSpec as P


CORES = 2

INV_SQRT_TWO = 0.7071067811865476
INV_SQRT_TWO_PI = 0.3989422804014327


def gelu_slope(values):
    return (
        0.5 * (1.0 + lax.erf(values * INV_SQRT_TWO))
        + values * jnp.exp(-0.5 * values * values) * INV_SQRT_TWO_PI
    )


def hop(block, pairs):
    return lax.ppermute(block, "tensor", pairs)


def traced(kept_input, kept_grad, up_weight_t, up_bias, down_weight, kept_count):
    slots = kept_input.shape[0]
    members = lax.axis_size("tensor")
    chips = members // CORES
    steps = chips // 2
    core = lax.axis_index("tensor") % CORES
    contract = (((1,), (1,)), ((), ()))
    sibling = [(i, i ^ 1) for i in range(members)]
    out = [
        (i, (i + (CORES if i % CORES == 0 else -CORES)) % members) for i in range(members)
    ]
    home = [(target, source) for source, target in out]
    out_far = [(source, target) for source, target in out if source % CORES == 0]
    home_far = [(target, source) for source, target in out_far]

    mine = jnp.stack((kept_input, kept_grad), axis=0)
    other = hop(mine, sibling)

    def both(block):
        return jnp.concatenate([block, hop(block, sibling)], axis=0)

    up = both(up_weight_t)
    down = both(down_weight)
    bias = both(up_bias).astype(jnp.float32)

    def terms(pieces):
        inputs = jnp.concatenate([piece[0] for piece in pieces], axis=0)
        out_grads = jnp.concatenate([piece[1] for piece in pieces], axis=0)
        preact = lax.dot_general(inputs, up, contract, preferred_element_type=jnp.float32) + bias
        down_grad = lax.dot_general(out_grads, down, contract, preferred_element_type=jnp.float32)
        pre_grad = (gelu_slope(preact) * down_grad).astype(jnp.bfloat16)
        pre_grad = lax.optimization_barrier(pre_grad)
        partials = jnp.dot(pre_grad, up, preferred_element_type=jnp.float32)
        partials = partials.astype(jnp.bfloat16)
        return [partials[i * slots : (i + 1) * slots] for i in range(len(pieces))]

    chain_mine, chain_other = [mine], [other]
    for step in range(1, steps + 1):
        pairs = out if step < steps else out_far
        if step == steps - 1:
            up, down, bias, chain_other[-1] = lax.optimization_barrier(
                (up, down, bias, chain_other[-1])
            )
        chain_mine.append(hop(chain_mine[-1], pairs))
        chain_other.append(hop(chain_other[-1], pairs))
    chain_mine[steps] = jnp.where(core == 0, chain_mine[steps], mine)
    chain_other[steps] = jnp.where(core == 0, chain_other[steps], other)

    near = terms(chain_mine[1:steps] + chain_other[1:steps])
    far_pieces, near = lax.optimization_barrier(
        ([chain_mine[steps], chain_other[steps]], near)
    )
    far = terms(far_pieces)
    for_mine = near[: steps - 1] + far[:1]
    for_other = near[steps - 1 :] + far[1:]

    def add(moved, part):
        return (moved.astype(jnp.float32) + part.astype(jnp.float32)).astype(jnp.bfloat16)

    sum_other = hop(for_other[-1], home_far)
    sum_mine = hop(for_mine[-1], home_far)
    for step in range(2, steps + 1):
        sum_other = hop(add(sum_other, for_other[steps - step]), home)
        sum_mine = hop(add(sum_mine, for_mine[steps - step]), home)
    kept_here = core == 1
    sum_other = sum_other.astype(jnp.float32) + jnp.where(kept_here, for_other[-1], 0.0)
    from_sibling = hop(sum_other.astype(jnp.bfloat16), sibling)
    branch = (
        sum_mine.astype(jnp.float32)
        + jnp.where(kept_here, for_mine[-1], 0.0).astype(jnp.float32)
        + from_sibling.astype(jnp.float32)
    ).astype(jnp.bfloat16)
    usable = jnp.arange(slots, dtype=jnp.int32) < kept_count[0]
    summed = kept_grad.astype(jnp.float32) + branch.astype(jnp.float32)
    return jnp.where(usable[:, None], summed, jnp.float32(0.0)).astype(jnp.bfloat16)


def solution(mesh):
    placed = (
        P(("dp", "tensor"), None),
        P(("dp", "tensor"), None),
        P("tensor", None),
        P("tensor"),
        P("tensor", None),
        P(("dp", "tensor")),
    )
    return jax.shard_map(
        traced, mesh=mesh, in_specs=placed, out_specs=P(("dp", "tensor"), None), check_vma=False
    )
```

```python
import jax
import jax.numpy as jnp
from jax import lax
from jax.sharding import PartitionSpec as P


CORES = 2

INV_SQRT_TWO = 0.7071067811865476
INV_SQRT_TWO_PI = 0.3989422804014327


def gelu_slope(values):
    return (
        0.5 * (1.0 + lax.erf(values * INV_SQRT_TWO))
        + values * jnp.exp(-0.5 * values * values) * INV_SQRT_TWO_PI
    )


def hop(block, pairs):
    return lax.ppermute(block, "tensor", pairs)


def traced(kept_input, kept_grad, up_weight_t, up_bias, down_weight, kept_count):
    slots = kept_input.shape[0]
    members = lax.axis_size("tensor")
    chips = members // CORES
    steps = chips // 2
    core = lax.axis_index("tensor") % CORES
    contract = (((1,), (1,)), ((), ()))
    sibling = [(i, i ^ 1) for i in range(members)]
    out = [
        (i, (i + (CORES if i % CORES == 0 else -CORES)) % members) for i in range(members)
    ]
    home = [(target, source) for source, target in out]
    out_far = [(source, target) for source, target in out if source % CORES == 0]
    home_far = [(target, source) for source, target in out_far]

    mine = jnp.stack((kept_input, kept_grad), axis=0)
    other = hop(mine, sibling)

    def both(block):
        theirs = hop(block, sibling)
        return lax.optimization_barrier(jnp.concatenate([block, theirs], axis=0))

    up = both(up_weight_t)
    down = both(down_weight)
    bias = both(up_bias).astype(jnp.float32)

    def terms(pieces):
        inputs = jnp.concatenate([piece[0] for piece in pieces], axis=0)
        out_grads = jnp.concatenate([piece[1] for piece in pieces], axis=0)
        preact = lax.dot_general(inputs, up, contract, preferred_element_type=jnp.float32) + bias
        down_grad = lax.dot_general(out_grads, down, contract, preferred_element_type=jnp.float32)
        pre_grad = (gelu_slope(preact) * down_grad).astype(jnp.bfloat16)
        pre_grad = lax.optimization_barrier(pre_grad)
        partials = jnp.dot(pre_grad, up, preferred_element_type=jnp.float32)
        partials = partials.astype(jnp.bfloat16)
        return [partials[i * slots : (i + 1) * slots] for i in range(len(pieces))]

    chain_mine, chain_other = [mine], [other]
    for step in range(1, steps + 1):
        pairs = out if step < steps else out_far
        chain_mine.append(hop(chain_mine[-1], pairs))
        chain_other.append(hop(chain_other[-1], pairs))
    chain_mine[steps] = jnp.where(core == 0, chain_mine[steps], mine)
    chain_other[steps] = jnp.where(core == 0, chain_other[steps], other)

    arrivals = [piece for pair in zip(chain_mine[1:steps], chain_other[1:steps]) for piece in pair]
    near = terms(arrivals)
    far_pieces, near = lax.optimization_barrier(
        ([chain_mine[steps], chain_other[steps]], near)
    )
    far = terms(far_pieces)
    for_mine = near[0::2] + far[:1]
    for_other = near[1::2] + far[1:]

    def add(moved, part):
        return (moved.astype(jnp.float32) + part.astype(jnp.float32)).astype(jnp.bfloat16)

    sum_other = hop(for_other[-1], home_far)
    sum_mine = hop(for_mine[-1], home_far)
    for step in range(2, steps + 1):
        sum_other = hop(add(sum_other, for_other[steps - step]), home)
        sum_mine = hop(add(sum_mine, for_mine[steps - step]), home)
    kept_here = core == 1
    sum_other = sum_other.astype(jnp.float32) + jnp.where(kept_here, for_other[-1], 0.0)
    from_sibling = hop(sum_other.astype(jnp.bfloat16), sibling)
    branch = (
        sum_mine.astype(jnp.float32)
        + jnp.where(kept_here, for_mine[-1], 0.0).astype(jnp.float32)
        + from_sibling.astype(jnp.float32)
    ).astype(jnp.bfloat16)
    usable = jnp.arange(slots, dtype=jnp.int32) < kept_count[0]
    summed = kept_grad.astype(jnp.float32) + branch.astype(jnp.float32)
    return jnp.where(usable[:, None], summed, jnp.float32(0.0)).astype(jnp.bfloat16)


def solution(mesh):
    placed = (
        P(("dp", "tensor"), None),
        P(("dp", "tensor"), None),
        P("tensor", None),
        P("tensor"),
        P("tensor", None),
        P(("dp", "tensor")),
    )
    return jax.shard_map(
        traced, mesh=mesh, in_specs=placed, out_specs=P(("dp", "tensor"), None), check_vma=False
    )
```

```python
import jax
import jax.numpy as jnp
from jax import lax
from jax.sharding import PartitionSpec as P


CORES = 2

INV_SQRT_TWO = 0.7071067811865476
INV_SQRT_TWO_PI = 0.3989422804014327


def gelu_slope(values):
    return (
        0.5 * (1.0 + lax.erf(values * INV_SQRT_TWO))
        + values * jnp.exp(-0.5 * values * values) * INV_SQRT_TWO_PI
    )


def hop(block, pairs):
    return lax.ppermute(block, "tensor", pairs)


def traced(kept_input, kept_grad, up_weight_t, up_bias, down_weight, kept_count):
    slots = kept_input.shape[0]
    members = lax.axis_size("tensor")
    chips = members // CORES
    steps = chips // 2
    core = lax.axis_index("tensor") % CORES
    contract = (((1,), (1,)), ((), ()))
    sibling = [(i, i ^ 1) for i in range(members)]
    out = [
        (i, (i + (CORES if i % CORES == 0 else -CORES)) % members) for i in range(members)
    ]
    home = [(target, source) for source, target in out]
    out_far = [(source, target) for source, target in out if source % CORES == 0]
    home_far = [(target, source) for source, target in out_far]
    out_cross = [(source ^ 1, target) for source, target in out]
    home_cross = [(target, source) for source, target in out_cross]
    to_second = [(i, i + 1) for i in range(0, members, CORES)]
    to_first = [(target, source) for source, target in to_second]

    mine = jnp.stack((kept_input, kept_grad), axis=0)
    other = hop(mine, to_second)

    def both(block):
        theirs = hop(block, sibling)
        return lax.optimization_barrier(jnp.concatenate([block, theirs], axis=0))

    up = both(up_weight_t)
    down = both(down_weight)
    bias = both(up_bias).astype(jnp.float32)

    def terms(pieces):
        inputs = jnp.concatenate([piece[0] for piece in pieces], axis=0)
        out_grads = jnp.concatenate([piece[1] for piece in pieces], axis=0)
        preact = lax.dot_general(inputs, up, contract, preferred_element_type=jnp.float32) + bias
        down_grad = lax.dot_general(out_grads, down, contract, preferred_element_type=jnp.float32)
        pre_grad = (gelu_slope(preact) * down_grad).astype(jnp.bfloat16)
        pre_grad = lax.optimization_barrier(pre_grad)
        partials = jnp.dot(pre_grad, up, preferred_element_type=jnp.float32)
        partials = partials.astype(jnp.bfloat16)
        return [partials[i * slots : (i + 1) * slots] for i in range(len(pieces))]

    chain_mine, chain_other = [mine], [mine]
    for step in range(1, steps + 1):
        pairs = out if step < steps else out_far
        chain_mine.append(hop(chain_mine[-1], pairs))
        crossing = out_cross if step == 1 else pairs
        chain_other.append(hop(chain_other[-1], crossing))
    chain_mine[steps] = jnp.where(core == 0, chain_mine[steps], mine)
    chain_other[steps] = jnp.where(core == 0, chain_other[steps], other)

    arrivals = [piece for pair in zip(chain_mine[1:steps], chain_other[1:steps]) for piece in pair]
    near = terms(arrivals)
    far_pieces, near = lax.optimization_barrier(
        ([chain_mine[steps], chain_other[steps]], near)
    )
    far = terms(far_pieces)
    for_mine = near[0::2] + far[:1]
    for_other = near[1::2] + far[1:]

    def add(moved, part):
        return (moved.astype(jnp.float32) + part.astype(jnp.float32)).astype(jnp.bfloat16)

    sum_other = hop(for_other[-1], home_far)
    sum_mine = hop(for_mine[-1], home_far)
    for step in range(2, steps + 1):
        crossing = home_cross if step == steps else home
        sum_other = hop(add(sum_other, for_other[steps - step]), crossing)
        sum_mine = hop(add(sum_mine, for_mine[steps - step]), home)
    kept = jnp.where(core == 1, for_mine[-1], 0.0).astype(jnp.float32)
    joined = hop(for_other[-1], to_first)
    branch = (
        sum_mine.astype(jnp.float32)
        + sum_other.astype(jnp.float32)
        + (kept + joined.astype(jnp.float32))
    ).astype(jnp.bfloat16)
    usable = jnp.arange(slots, dtype=jnp.int32) < kept_count[0]
    summed = kept_grad.astype(jnp.float32) + branch.astype(jnp.float32)
    return jnp.where(usable[:, None], summed, jnp.float32(0.0)).astype(jnp.bfloat16)


def solution(mesh):
    placed = (
        P(("dp", "tensor"), None),
        P(("dp", "tensor"), None),
        P("tensor", None),
        P("tensor"),
        P("tensor", None),
        P(("dp", "tensor")),
    )
    return jax.shard_map(
        traced, mesh=mesh, in_specs=placed, out_specs=P(("dp", "tensor"), None), check_vma=False
    )
```

```python
import jax
import jax.numpy as jnp
from jax import lax
from jax.sharding import PartitionSpec as P


CORES = 2
CHAINS = 3

INV_SQRT_TWO = 0.7071067811865476
INV_SQRT_TWO_PI = 0.3989422804014327


def gelu_slope(values):
    return (
        0.5 * (1.0 + lax.erf(values * INV_SQRT_TWO))
        + values * jnp.exp(-0.5 * values * values) * INV_SQRT_TWO_PI
    )


def hop(block, pairs):
    return lax.ppermute(block, "tensor", pairs)


def traced(kept_input, kept_grad, up_weight_t, up_bias, down_weight, kept_count):
    slots = kept_input.shape[0]
    members = lax.axis_size("tensor")
    chips = members // CORES
    steps = chips // 2
    core = lax.axis_index("tensor") % CORES
    contract = (((1,), (1,)), ((), ()))
    sibling = [(i, i ^ 1) for i in range(members)]
    out = [
        (i, (i + (CORES if i % CORES == 0 else -CORES)) % members) for i in range(members)
    ]
    home = [(target, source) for source, target in out]
    out_far = [(source, target) for source, target in out if source % CORES == 0]
    home_far = [(target, source) for source, target in out_far]
    home_cross = [(source, target ^ 1) for source, target in home]
    to_first = [(i + 1, i) for i in range(0, members, CORES)]
    part = 2 * slots // CHAINS

    mine = jnp.stack((kept_input, kept_grad), axis=0)
    other = hop(mine, sibling)

    def both(block):
        theirs = hop(block, sibling)
        return lax.optimization_barrier(jnp.concatenate([block, theirs], axis=0))

    up = both(up_weight_t)
    down = both(down_weight)
    bias = both(up_bias).astype(jnp.float32)

    def terms(pieces):
        inputs = jnp.concatenate([piece[0] for piece in pieces], axis=0)
        out_grads = jnp.concatenate([piece[1] for piece in pieces], axis=0)
        preact = lax.dot_general(inputs, up, contract, preferred_element_type=jnp.float32) + bias
        down_grad = lax.dot_general(out_grads, down, contract, preferred_element_type=jnp.float32)
        pre_grad = (gelu_slope(preact) * down_grad).astype(jnp.bfloat16)
        pre_grad = lax.optimization_barrier(pre_grad)
        partials = jnp.dot(pre_grad, up, preferred_element_type=jnp.float32)
        partials = partials.astype(jnp.bfloat16)
        return [partials[i * part : (i + 1) * part] for i in range(len(pieces))]

    middle = jnp.concatenate([mine[:, part:], other[:, : 2 * part - slots]], axis=1)
    start = [mine[:, :part], middle, other[:, 2 * part - slots :]]
    chains = [[piece] for piece in start]
    for step in range(1, steps + 1):
        pairs = out if step < steps else out_far
        for chain in chains:
            chain.append(hop(chain[-1], pairs))
    last = [jnp.where(core == 0, chain[steps], piece) for chain, piece in zip(chains, start)]

    arrivals = [chain[step] for step in range(1, steps) for chain in chains]
    near = terms(arrivals)
    last, near = lax.optimization_barrier((last, near))
    far = terms(last)

    def add(moved, term):
        return (moved.astype(jnp.float32) + term.astype(jnp.float32)).astype(jnp.bfloat16)

    sums = [hop(term, home_far) for term in far]
    for step in range(2, steps + 1):
        group = near[CHAINS * (steps - step) : CHAINS * (steps - step + 1)]
        totals = [add(moved, term) for moved, term in zip(sums, group)]
        if step < steps:
            sums = [hop(total, home) for total in totals]
    seam = slots - part
    mine_sum = jnp.concatenate([hop(totals[0], home), hop(totals[1][:seam], home)], axis=0)
    other_sum = jnp.concatenate(
        [hop(totals[1][seam:], home_cross), hop(totals[2], home_cross)], axis=0
    )
    worked = jnp.concatenate(far, axis=0)
    kept = jnp.where(core == 1, worked[:slots], 0.0).astype(jnp.float32)
    joined = hop(worked[slots:], to_first)
    branch = (
        mine_sum.astype(jnp.float32)
        + other_sum.astype(jnp.float32)
        + (kept + joined.astype(jnp.float32))
    ).astype(jnp.bfloat16)
    usable = jnp.arange(slots, dtype=jnp.int32) < kept_count[0]
    summed = kept_grad.astype(jnp.float32) + branch.astype(jnp.float32)
    return jnp.where(usable[:, None], summed, jnp.float32(0.0)).astype(jnp.bfloat16)


def solution(mesh):
    placed = (
        P(("dp", "tensor"), None),
        P(("dp", "tensor"), None),
        P("tensor", None),
        P("tensor"),
        P("tensor", None),
        P(("dp", "tensor")),
    )
    return jax.shard_map(
        traced, mesh=mesh, in_specs=placed, out_specs=P(("dp", "tensor"), None), check_vma=False
    )
```

```python
import jax
import jax.numpy as jnp
from jax import lax
from jax.sharding import PartitionSpec as P


CORES = 2

INV_SQRT_TWO = 0.7071067811865476
INV_SQRT_TWO_PI = 0.3989422804014327


def gelu_slope(values):
    return (
        0.5 * (1.0 + lax.erf(values * INV_SQRT_TWO))
        + values * jnp.exp(-0.5 * values * values) * INV_SQRT_TWO_PI
    )


def hop(block, pairs):
    return lax.ppermute(block, "tensor", pairs)


def traced(kept_input, kept_grad, up_weight_t, up_bias, down_weight, kept_count):
    slots = kept_input.shape[0]
    members = lax.axis_size("tensor")
    chips = members // CORES
    steps = chips // 2
    core = lax.axis_index("tensor") % CORES
    contract = (((1,), (1,)), ((), ()))
    sibling = [(i, i ^ 1) for i in range(members)]
    out = [
        (i, (i + (CORES if i % CORES == 0 else -CORES)) % members) for i in range(members)
    ]
    home = [(target, source) for source, target in out]
    out_far = [(source, target) for source, target in out if source % CORES == 0]
    home_far = [(target, source) for source, target in out_far]
    home_cross = [(source, target ^ 1) for source, target in home]
    to_first = [(i + 1, i) for i in range(0, members, CORES)]

    mine = jnp.stack((kept_input, kept_grad), axis=0)
    other = hop(mine, sibling)

    def both(block):
        theirs = hop(block, sibling)
        return lax.optimization_barrier(jnp.concatenate([block, theirs], axis=0))

    up = both(up_weight_t)
    down = both(down_weight)
    bias = both(up_bias).astype(jnp.float32)

    def terms(pieces):
        inputs = jnp.concatenate([piece[0] for piece in pieces], axis=0)
        out_grads = jnp.concatenate([piece[1] for piece in pieces], axis=0)
        preact = lax.optimization_barrier(
            lax.dot_general(inputs, up, contract, preferred_element_type=jnp.float32)
            + bias
        )
        down_grad = lax.dot_general(out_grads, down, contract, preferred_element_type=jnp.float32)
        pre_grad = (gelu_slope(preact) * down_grad).astype(jnp.bfloat16)
        pre_grad = lax.optimization_barrier(pre_grad)
        partials = jnp.dot(pre_grad, up, preferred_element_type=jnp.float32)
        partials = partials.astype(jnp.bfloat16)
        return [partials[i * slots : (i + 1) * slots] for i in range(len(pieces))]

    chain_mine, chain_other = [mine], [other]
    for step in range(1, steps + 1):
        pairs = out if step < steps else out_far
        chain_mine.append(hop(chain_mine[-1], pairs))
        chain_other.append(hop(chain_other[-1], pairs))
    chain_mine[steps] = jnp.where(core == 0, chain_mine[steps], mine)
    chain_other[steps] = jnp.where(core == 0, chain_other[steps], other)

    arrivals = [piece for pair in zip(chain_mine[1:steps], chain_other[1:steps]) for piece in pair]
    near = lax.optimization_barrier(terms(arrivals[:-1]))
    (far_mine,) = terms(chain_mine[steps:])
    late_other, far_other = lax.optimization_barrier(terms([arrivals[-1], chain_other[steps]]))
    for_mine = near[0::2] + [far_mine]
    for_other = near[1::2] + [late_other, far_other]

    def add(moved, part):
        return (moved.astype(jnp.float32) + part.astype(jnp.float32)).astype(jnp.bfloat16)

    sum_mine = hop(for_mine[-1], home_far)
    sum_other = hop(for_other[-1], home_far)
    for step in range(2, steps + 1):
        crossing = home_cross if step == steps else home
        sum_mine = hop(add(sum_mine, for_mine[steps - step]), home)
        sum_other = hop(add(sum_other, for_other[steps - step]), crossing)
    kept = jnp.where(core == 1, for_mine[-1], 0.0).astype(jnp.float32)
    joined = hop(for_other[-1], to_first)
    branch = (
        sum_mine.astype(jnp.float32)
        + sum_other.astype(jnp.float32)
        + (kept + joined.astype(jnp.float32))
    ).astype(jnp.bfloat16)
    usable = jnp.arange(slots, dtype=jnp.int32) < kept_count[0]
    summed = kept_grad.astype(jnp.float32) + branch.astype(jnp.float32)
    return jnp.where(usable[:, None], summed, jnp.float32(0.0)).astype(jnp.bfloat16)


def solution(mesh):
    placed = (
        P(("dp", "tensor"), None),
        P(("dp", "tensor"), None),
        P("tensor", None),
        P("tensor"),
        P("tensor", None),
        P(("dp", "tensor")),
    )
    return jax.shard_map(
        traced, mesh=mesh, in_specs=placed, out_specs=P(("dp", "tensor"), None), check_vma=False
    )
```

```python
import jax
import jax.numpy as jnp
from jax import lax
from jax.sharding import PartitionSpec as P


CORES = 2

INV_SQRT_TWO = 0.7071067811865476
INV_SQRT_TWO_PI = 0.3989422804014327


def gelu_slope(values):
    return (
        0.5 * (1.0 + lax.erf(values * INV_SQRT_TWO))
        + values * jnp.exp(-0.5 * values * values) * INV_SQRT_TWO_PI
    )


def hop(block, pairs):
    return lax.ppermute(block, "tensor", pairs)


def traced(kept_input, kept_grad, up_weight_t, up_bias, down_weight, kept_count):
    slots = kept_input.shape[0]
    members = lax.axis_size("tensor")
    chips = members // CORES
    steps = chips // 2
    core = lax.axis_index("tensor") % CORES
    contract = (((1,), (1,)), ((), ()))
    sibling = [(i, i ^ 1) for i in range(members)]
    out = [
        (i, (i + (CORES if i % CORES == 0 else -CORES)) % members) for i in range(members)
    ]
    home = [(target, source) for source, target in out]
    out_far = [(source, target) for source, target in out if source % CORES == 0]
    home_far = [(target, source) for source, target in out_far]
    home_cross = [(source, target ^ 1) for source, target in home]
    out_cross = [(source ^ 1, target) for source, target in out]
    to_first = [(i + 1, i) for i in range(0, members, CORES)]
    to_second = [(target, source) for source, target in to_first]

    mine = jnp.stack((kept_input, kept_grad), axis=0)
    other = hop(mine, to_second)

    def both(block):
        theirs = hop(block, sibling)
        return lax.optimization_barrier(jnp.concatenate([block, theirs], axis=0))

    up = both(up_weight_t)
    down = both(down_weight)
    bias = both(up_bias).astype(jnp.float32)

    def terms(pieces):
        inputs = jnp.concatenate([piece[0] for piece in pieces], axis=0)
        out_grads = jnp.concatenate([piece[1] for piece in pieces], axis=0)
        preact = lax.optimization_barrier(
            lax.dot_general(inputs, up, contract, preferred_element_type=jnp.float32)
            + bias
        )
        down_grad = lax.dot_general(out_grads, down, contract, preferred_element_type=jnp.float32)
        pre_grad = (gelu_slope(preact) * down_grad).astype(jnp.bfloat16)
        pre_grad = lax.optimization_barrier(pre_grad)
        partials = jnp.dot(pre_grad, up, preferred_element_type=jnp.float32)
        partials = partials.astype(jnp.bfloat16)
        return [partials[i * slots : (i + 1) * slots] for i in range(len(pieces))]

    chain_mine, chain_other = [mine], [mine]
    for step in range(1, steps + 1):
        pairs = out if step < steps else out_far
        chain_mine.append(hop(chain_mine[-1], pairs))
        crossing = out_cross if step == 1 else pairs
        chain_other.append(hop(chain_other[-1], crossing))
    chain_mine[steps] = jnp.where(core == 0, chain_mine[steps], mine)
    chain_other[steps] = jnp.where(core == 0, chain_other[steps], other)

    arrivals = [piece for pair in zip(chain_mine[1:steps], chain_other[1:steps]) for piece in pair]
    near = terms(arrivals[:-1])
    far_pieces, near = lax.optimization_barrier(
        ([arrivals[-1], chain_mine[steps], chain_other[steps]], near)
    )
    far = terms(far_pieces)
    for_mine = near[0::2] + far[1:2]
    for_other = near[1::2] + far[0::2]

    def add(moved, part):
        return (moved.astype(jnp.float32) + part.astype(jnp.float32)).astype(jnp.bfloat16)

    sum_other = hop(for_other[-1], home_far)
    sum_mine = hop(for_mine[-1], home_far)
    for step in range(2, steps + 1):
        crossing = home_cross if step == steps else home
        sum_other = hop(add(sum_other, for_other[steps - step]), crossing)
        sum_mine = hop(add(sum_mine, for_mine[steps - step]), home)
    kept = jnp.where(core == 1, for_mine[-1], 0.0).astype(jnp.float32)
    joined = hop(for_other[-1], to_first)
    branch = (
        sum_mine.astype(jnp.float32)
        + sum_other.astype(jnp.float32)
        + (kept + joined.astype(jnp.float32))
    ).astype(jnp.bfloat16)
    usable = jnp.arange(slots, dtype=jnp.int32) < kept_count[0]
    summed = kept_grad.astype(jnp.float32) + branch.astype(jnp.float32)
    return jnp.where(usable[:, None], summed, jnp.float32(0.0)).astype(jnp.bfloat16)


def solution(mesh):
    placed = (
        P(("dp", "tensor"), None),
        P(("dp", "tensor"), None),
        P("tensor", None),
        P("tensor"),
        P("tensor", None),
        P(("dp", "tensor")),
    )
    return jax.shard_map(
        traced, mesh=mesh, in_specs=placed, out_specs=P(("dp", "tensor"), None), check_vma=False
    )
```

```python
import jax
import jax.numpy as jnp
from jax import lax
from jax.sharding import PartitionSpec as P


CORES = 2

INV_SQRT_TWO = 0.7071067811865476
INV_SQRT_TWO_PI = 0.3989422804014327


def gelu_slope(values):
    return (
        0.5 * (1.0 + lax.erf(values * INV_SQRT_TWO))
        + values * jnp.exp(-0.5 * values * values) * INV_SQRT_TWO_PI
    )


def hop(block, pairs):
    return lax.ppermute(block, "tensor", pairs)


def traced(kept_input, kept_grad, up_weight_t, up_bias, down_weight, kept_count):
    slots = kept_input.shape[0]
    members = lax.axis_size("tensor")
    chips = members // CORES
    steps = chips // 2
    core = lax.axis_index("tensor") % CORES
    contract = (((1,), (1,)), ((), ()))
    sibling = [(i, i ^ 1) for i in range(members)]
    out = [
        (i, (i + (CORES if i % CORES == 0 else -CORES)) % members) for i in range(members)
    ]
    home = [(target, source) for source, target in out]
    out_far = [(source, target) for source, target in out if source % CORES == 0]
    home_far = [(target, source) for source, target in out_far]
    home_cross = [(source, target ^ 1) for source, target in home]
    to_first = [(i + 1, i) for i in range(0, members, CORES)]

    mine = jnp.stack((kept_input, kept_grad), axis=0)
    other = hop(mine, sibling)

    def both(block):
        theirs = hop(block, sibling)
        return lax.optimization_barrier(jnp.concatenate([block, theirs], axis=0))

    up = both(up_weight_t)
    down = both(down_weight)
    bias = both(up_bias).astype(jnp.float32)

    def terms(pieces):
        inputs = jnp.concatenate([piece[0] for piece in pieces], axis=0)
        out_grads = jnp.concatenate([piece[1] for piece in pieces], axis=0)
        preact = lax.optimization_barrier(
            lax.dot_general(inputs, up, contract, preferred_element_type=jnp.float32)
            + bias
        )
        down_grad = lax.dot_general(out_grads, down, contract, preferred_element_type=jnp.float32)
        pre_grad = (gelu_slope(preact) * down_grad).astype(jnp.bfloat16)
        pre_grad = lax.optimization_barrier(pre_grad)
        partials = jnp.dot(pre_grad, up, preferred_element_type=jnp.float32)
        partials = partials.astype(jnp.bfloat16)
        return [partials[i * slots : (i + 1) * slots] for i in range(len(pieces))]

    chain_mine, chain_other = [mine], [other]
    for step in range(1, steps + 1):
        pairs = out if step < steps else out_far
        chain_mine.append(hop(chain_mine[-1], pairs))
        chain_other.append(hop(chain_other[-1], pairs))
    chain_mine[steps] = jnp.where(core == 0, chain_mine[steps], mine)
    chain_other[steps] = jnp.where(core == 0, chain_other[steps], other)

    arrivals = [piece for pair in zip(chain_mine[1:steps], chain_other[1:steps]) for piece in pair]
    near = terms(arrivals[:-1])
    far_pieces, near = lax.optimization_barrier(
        ([arrivals[-1], chain_mine[steps], chain_other[steps]], near)
    )
    far = terms(far_pieces)
    for_mine = near[0::2] + far[1:2]
    for_other = near[1::2] + far[0::2]

    def add(moved, part):
        return (moved.astype(jnp.float32) + part.astype(jnp.float32)).astype(jnp.bfloat16)

    sum_other = hop(for_other[-1], home_far)
    sum_mine = hop(for_mine[-1], home_far)
    for step in range(2, steps + 1):
        crossing = home_cross if step == steps else home
        sum_other = hop(add(sum_other, for_other[steps - step]), crossing)
        sum_mine = hop(add(sum_mine, for_mine[steps - step]), home)
    kept = jnp.where(core == 1, for_mine[-1], 0.0).astype(jnp.float32)
    joined = hop(for_other[-1], to_first)
    branch = (
        sum_mine.astype(jnp.float32)
        + sum_other.astype(jnp.float32)
        + (kept + joined.astype(jnp.float32))
    ).astype(jnp.bfloat16)
    usable = jnp.arange(slots, dtype=jnp.int32) < kept_count[0]
    summed = kept_grad.astype(jnp.float32) + branch.astype(jnp.float32)
    return jnp.where(usable[:, None], summed, jnp.float32(0.0)).astype(jnp.bfloat16)


def solution(mesh):
    placed = (
        P(("dp", "tensor"), None),
        P(("dp", "tensor"), None),
        P("tensor", None),
        P("tensor"),
        P("tensor", None),
        P(("dp", "tensor")),
    )
    return jax.shard_map(
        traced, mesh=mesh, in_specs=placed, out_specs=P(("dp", "tensor"), None), check_vma=False
    )
```
